32 devices in a mesh: prow: 8 (over z, x), pcol: 4 (over y, core).
Axes of the slice: x: 2, y: 2, z: 4, core: 2. Of those that a mesh axis runs over, the one named last changes fastest.
Arguments:
- panel: float32 [8192, 128], P('prow'), may hold values from -1.8765018 to 11.876502
- trailing: float32 [8192, 8192], P('prow', 'pcol'), may hold values from -8 to 8
Outputs:
- updated: float32 [8192, 8192], P('prow', 'pcol')
- band_block: float32 [128, 128], replicated
The draws below stay inside these ranges and needn't reach their ends.
All inputs are finite; a program needn't handle non-finite values.
Results may differ from the reference program's by a relative error of at most 0.00012.
Values sent between devices are 32-bit elements; how exact they have to be, the bound alone decides.
A program may use at most 128 MiB of HBM per device.

```python
import jax
import jax.numpy as jnp
from jax import lax

PANEL = 128
ORDER = 8192


def draw_panel(key, part):
    keys = jax.random.split(jax.random.fold_in(key, 11), 3)
    position = jnp.arange(ORDER, dtype=jnp.float32) / ORDER
    row_scale = jnp.power(3.0, position) * jnp.power(10.0, jax.random.uniform(keys[0], (ORDER,), jnp.float32))
    col_scale = jnp.power(10.0, jax.random.uniform(keys[1], (PANEL,), jnp.float32))
    rough = jnp.clip(jax.random.normal(keys[2], (ORDER, PANEL), jnp.float32), -5.0, 5.0)
    values = rough * row_scale[:, None] * col_scale[None, :] / jnp.sqrt(78.0 * ORDER)
    rows = jnp.arange(ORDER)[:, None]
    cols = jnp.arange(PANEL)[None, :]
    values = values + jnp.where(rows == cols, col_scale[None, :], 0.0)
    return values.astype(jnp.float32)


def draw_trailing(key, part):
    inner = jax.random.fold_in(key, 23)
    source = jnp.clip(jax.random.normal(inner, (ORDER, ORDER), jnp.float32), -5.0, 5.0)
    return ((source + source.T) * 0.7071).astype(jnp.float32)


def setup_inputs(seed: int = 0) -> dict:
    seeds = jax.random.split(jax.random.key(seed), 3)
    return {
        "panel": draw_panel(jax.random.fold_in(seeds[2], 71), 0),
        "trailing": draw_trailing(jax.random.fold_in(seeds[2], 71), 0),
    }


def hdot(left, right):
    return jnp.dot(left.astype(jnp.float32), right.astype(jnp.float32), precision=lax.Precision.HIGHEST, preferred_element_type=jnp.float32)

def reference(panel, trailing):
    gram = hdot(panel.T, panel)
    lower = jnp.linalg.cholesky(gram)
    basis = jax.scipy.linalg.solve_triangular(lower, panel.T, lower=True).T
    head = basis[:PANEL]
    identity_mat = jnp.eye(PANEL, dtype=jnp.float32)
    coupling = jnp.linalg.solve(identity_mat + head.T, identity_mat)
    unit = jnp.concatenate([identity_mat, jnp.zeros((ORDER - PANEL, PANEL), jnp.float32)], axis=0)
    vectors = basis + unit
    mixed = hdot(hdot(trailing, vectors), coupling)
    small = hdot(coupling.T, hdot(vectors.T, mixed))
    update = mixed - 0.5 * hdot(vectors, small)
    updated = trailing - hdot(vectors, update.T) - hdot(update, vectors.T)
    return (updated, -lower.T)
```

```python
import functools

import jax
import jax.numpy as jnp
from jax import lax
from jax.experimental import pallas as pl
from jax.experimental.pallas import tpu as pltpu
from jax.sharding import PartitionSpec as P

STEPS = 16


def factor_body(gram, top_t, between):
    size = gram.shape[0]
    rows = lax.broadcasted_iota(jnp.int32, (size, size), 0)
    cols = lax.broadcasted_iota(jnp.int32, (size, size), 1)

    def block(turn, carry):
        work, other = carry
        live = size - turn * STEPS
        for k in range(STEPS):
            if k % (STEPS // 2) == 0:
                between(2 * turn + 2 * k // STEPS)
            at_col = cols == k
            below = jnp.logical_and(rows > k, rows < live)
            col = jnp.broadcast_to(work[:, k : k + 1], (size, size))
            row_scale = lax.rsqrt(col[k : k + 1, :])
            row = jnp.where(at_col[:1], 1.0, work[k : k + 1, :]) * row_scale
            low = jnp.where(jnp.logical_and(rows >= k, rows < live), col * row_scale, 0.0)
            work = jnp.where(
                rows == k,
                row,
                jnp.where(below, jnp.where(at_col, 0.0, work) - low * row, work),
            )
            ocol = jnp.broadcast_to(other[:, k : k + 1], (size, size)) + low
            inv = 1.0 / ocol[k : k + 1, :]
            orow = jnp.where(at_col[:1], 1.0, other[k : k + 1, :]) * inv
            other = jnp.where(
                rows == k, orow, jnp.where(at_col, 0.0, other) - ocol * orow
            )
        work = jnp.concatenate([work[STEPS:], work[:STEPS]], axis=0)
        other = jnp.concatenate([other[STEPS:], other[:STEPS]], axis=0)
        return pltpu.roll(work, size - STEPS, 1), pltpu.roll(other, size - STEPS, 1)

    return lax.fori_loop(0, size // STEPS, block, (gram, top_t))


def split_factor(work, other):
    size = work.shape[0]
    rows = lax.broadcasted_iota(jnp.int32, (size, size), 0)
    cols = lax.broadcasted_iota(jnp.int32, (size, size), 1)
    linv = jnp.where(rows >= cols, work, 0.0)
    upper = jnp.where(rows < cols, work, jnp.where(rows == cols, 1.0 / jnp.where(rows == cols, work, 1.0), 0.0))
    coupling = lax.dot_general(
        other, upper, (((1,), (1,)), ((), ())), precision=lax.Precision.HIGHEST, preferred_element_type=jnp.float32
    )
    return linv, upper, coupling

MESH = pl.DeviceIdType.MESH
CHUNKS = 16
EARLY = (2, 5, 5)
SLACK = 2
TILE = 256
PAIR = 4
GRANT = 24 * 1024 * 1024
F32 = jnp.float32


def exact_dot(left, right, dims):
    return lax.dot_general(
        left, right, (dims, ((), ())), precision=lax.Precision.HIGHEST, preferred_element_type=F32
    )


def split(value):
    high = value.astype(jnp.bfloat16)
    return high, (value - high.astype(F32)).astype(jnp.bfloat16)


def pair_dot(left, right, dims):
    (lh, ll), (rh, rl) = left, right

    def one(a, b):
        return lax.dot_general(a, b, (dims, ((), ())), preferred_element_type=F32)

    return one(lh, rh) + (one(lh, rl) + one(ll, rh))


def exchange_kernel(
    sizes, panel_hbm, trail_ref, left_hi, left_lo, right_hi, right_lo, band_ref, t_buf,
    panel_ref, p_sem, own_sem, t_sem, colp, colq, vcat, part, acc, got, prod, vec,
    gram_ref, rs_ref, both, small_ref, rs2_ref, pc_ref, both2,
    top_send, top_recv, rs_send, rs_recv, ag_send, ag_recv, rs2_send, rs2_recv, ag2_send, ag2_recv, pc_send, pc_recv,
    pump_send, pump_recv, pump2_send, pump2_recv, red_send, red_recv, bit_send, bit_recv, back_send, back_recv,
):
    n, m, nx, blocks = sizes
    nz = n // nx
    rows, size = panel_ref.shape
    piece = size // n
    half = rows // 2
    chunk_rows = rows // CHUNKS
    me = lax.axis_index("prow")
    q = lax.axis_index("pcol")
    z, x = me // nx, me % nx
    bits = m.bit_length() - 1

    def flip(bit):
        step = 1 << bit
        return q + step - 2 * step * ((q // step) % 2)

    def peer(offset):
        return (me + offset) % n

    def remote(src, dst, send, recv, where):
        return pltpu.make_async_remote_copy(
            src_ref=src, dst_ref=dst, send_sem=send, recv_sem=recv, device_id=where, device_id_type=MESH
        )

    t_copy = pltpu.make_async_copy(trail_ref, t_buf, t_sem)
    p_copy = pltpu.make_async_copy(panel_hbm, panel_ref, p_sem)
    p_copy.start()
    t_copy.start()
    barrier = pltpu.get_barrier_semaphore()
    for offset in range(1, n):
        pl.semaphore_signal(barrier, inc=1, device_id={"prow": peer(offset)}, device_id_type=MESH)
    for offset in range(1, m):
        pl.semaphore_signal(barrier, inc=1, device_id={"pcol": (q + offset) % m}, device_id_type=MESH)

    def place(k):
        b = q * blocks + k
        return b, z - b // nx, x - b % nx

    def filled(buf, source):
        copies = []
        for k in range(blocks):
            b, _, _ = place(k)
            copies.append((me == b, pltpu.make_async_copy(source, buf.at[pl.ds(k * rows, rows)], own_sem)))
        return copies

    def fill(buf, source):
        for mine, copy in filled(buf, source):
            pl.when(mine)(copy.start)

    def fill_wait(buf, source):
        for mine, copy in filled(buf, source):
            pl.when(mine)(copy.wait)

    p_copy.wait()
    fill(colp, panel_ref)
    fill_wait(colp, panel_ref)
    pl.semaphore_wait(barrier, n - 1 + m - 1)

    def children(dz, dx):
        return (
            (jnp.logical_and(jnp.logical_and(dx == 0, dz >= 0), z < nz - 1), me + nx),
            (jnp.logical_and(jnp.logical_and(dx == 0, dz <= 0), z > 0), me - nx),
            (jnp.logical_and(dx >= 0, x < nx - 1), me + 1),
            (jnp.logical_and(dx <= 0, x > 0), me - 1),
        )

    def relays(dz, dx):
        flags = [has for has, _ in children(dz, dx)]
        return functools.reduce(jnp.logical_or, flags)

    def in_order(k, c):
        return pl.multiple_of(c * chunk_rows, chunk_rows)

    def paired(k, c):
        first = place(k)[0] // blocks % 2
        side = (first + c % PAIR // (PAIR // 2)) % 2
        at = side * half + c // PAIR * (PAIR // 2) * chunk_rows + c % (PAIR // 2) * chunk_rows
        return pl.multiple_of(at, chunk_rows)

    def settle(buf, send, recv, where, span):
        for k in range(blocks):
            _, dz, dx = place(k)
            away = jnp.logical_or(dz != 0, dx != 0)

            @pl.when(jnp.logical_and(away, jnp.logical_not(relays(dz, dx))))
            def _():
                for c in span:
                    part_of = buf.at[pl.ds(k * rows + where(k, c), chunk_rows)]
                    remote(part_of, part_of, send.at[k, 0], recv.at[k, c], {"prow": peer(1)}).wait_recv()

    def pump(step, buf, source, send, recv, where):
        for k in range(blocks):
            _, dz, dx = place(k)
            far = jnp.where(dz < 0, -dz, dz) + jnp.where(dx < 0, -dx, dx)
            c = step - SLACK * far

            @pl.when(jnp.logical_and(c >= 0, c < CHUNKS))
            def _():
                part_of = buf.at[pl.ds(k * rows + where(k, c), chunk_rows)]

                @pl.when(jnp.logical_and(far > 0, relays(dz, dx)))
                def _():
                    remote(part_of, part_of, send.at[k, 0], recv.at[k, c], {"prow": peer(1)}).wait_recv()

                for d, (has, to) in enumerate(children(dz, dx)):

                    @pl.when(jnp.logical_and(has, far > 0))
                    def _():
                        remote(part_of, part_of, send.at[k, d], recv.at[k, c], {"prow": to}).start()

                    @pl.when(jnp.logical_and(has, far == 0))
                    def _():
                        own = source.at[pl.ds(where(k, c), chunk_rows)]
                        remote(own, part_of, send.at[k, d], recv.at[k, c], {"prow": to}).start()

    def pump_p(step):
        pump(step, colp, panel_ref, pump_send, pump_recv, in_order)

    def pump_q(step):
        pump(step, colq, prod, pump2_send, pump2_recv, paired)

    def drain(buf, send, recv):
        for k in range(blocks):
            _, dz, dx = place(k)
            whole = buf.at[pl.ds(k * rows, rows)]
            for d, (has, to) in enumerate(children(dz, dx)):

                @pl.when(has)
                def _():
                    remote(whole, whole, send.at[k, d], recv.at[k, 0], {"prow": peer(1)}).wait_send()

    total_steps = CHUNKS + SLACK * (nz - 1 + max(nx - 2, 0))

    def scatter(src, slots, send, recv):
        def copy(offset):
            to = peer(offset)
            return remote(
                src.at[pl.ds(to * piece, piece)], slots.at[offset], send.at[offset], recv.at[offset], {"prow": to}
            )

        return [copy(offset) for offset in range(1, n)]

    def spread(slots, send, recv):
        def copy(offset):
            return remote(slots.at[me], slots.at[me], send.at[offset], recv.at[offset], {"prow": peer(offset)})

        def arrive(offset):
            slot = slots.at[peer(n - offset)]
            return remote(slot, slot, send.at[offset], recv.at[offset], {"prow": peer(offset)})

        return [copy(o) for o in range(1, n)], [arrive(o) for o in range(1, n)]

    def collected(src, slots):
        value = src[pl.ds(me * piece, piece)]
        for offset in range(1, n):
            value = value + slots[offset]
        return value

    def top_copy(j):
        return remote(panel_ref.at[pl.ds(j * piece, piece)], both.at[j, 1], top_send.at[j], top_recv, {"prow": j})

    @pl.when(me == 0)
    def _():
        for j in range(1, n):
            top_copy(j).start()
        both[0, 1] = panel_ref[:piece]

    for step in range(EARLY[0]):
        pump_p(step)
    gram_ref[...] = exact_dot(panel_ref[...], panel_ref[...], ((0,), (0,)))
    sends = scatter(gram_ref, rs_ref, rs_send, rs_recv)
    for copy in sends:
        copy.start()
    for step in range(EARLY[0], sum(EARLY[:2])):
        pump_p(step)

    @pl.when(me > 0)
    def _():
        slot = both.at[me, 1]
        remote(slot, slot, top_send.at[0], top_recv, {"prow": peer(1)}).wait_recv()

    for copy in sends:
        copy.wait_recv()
    both[me, 0] = collected(gram_ref, rs_ref)
    sends2, arrivals = spread(both, ag_send, ag_recv)
    for copy in sends2:
        copy.start()
    for step in range(sum(EARLY[:2]), sum(EARLY)):
        pump_p(step)
    for copy in arrivals:
        copy.wait_recv()
    for copy in sends + sends2:
        copy.wait_send()

    @pl.when(me == 0)
    def _():
        for j in range(1, n):
            top_copy(j).wait_send()

    done = sum(EARLY)
    turns = 2 * (size // STEPS)
    work, other = factor_body(
        both[:, 0].reshape(size, size),
        both[:, 1].reshape(size, size).T,
        lambda turn: pump_p(done + turn),
    )
    for step in range(done + turns, total_steps):
        pump_p(step)
    settle(colp, pump_send, pump_recv, in_order, range(CHUNKS))
    linv, upper, coupling = split_factor(work, other)
    band_ref[...] = -upper
    linv_pair = split(linv)

    def unit(start):
        r = lax.broadcasted_iota(jnp.int32, (TILE, size), 0) + start
        return jnp.where(r == lax.broadcasted_iota(jnp.int32, (TILE, size), 1), 1.0, 0.0)

    def col_vectors(i, carry):
        at = pl.ds(pl.multiple_of(i * TILE, TILE), TILE)
        value = pair_dot(split(colp[at]), linv_pair, ((1,), (1,))) + unit(q * blocks * rows + i * TILE)
        high, low = split(value)
        vcat[at, :size] = high
        vcat[at, size:] = low
        right_hi[at, size:] = high
        right_lo[at, size:] = low
        return carry

    lax.fori_loop(0, blocks * rows // TILE, col_vectors, 0)
    t_copy.wait()

    h = q % 2
    per_half = half // TILE
    mate = {"pcol": flip(0)}

    def half_at(side, i):
        return pl.ds(pl.multiple_of(side * half + i * TILE, TILE), TILE)

    def tile_of(i):
        return pl.ds(pl.multiple_of(i * TILE, TILE), TILE)

    def red_copy(i):
        return remote(part.at[half_at(1 - h, i)], got.at[0, tile_of(i)], red_send.at[i], red_recv.at[i], mate)

    def times(side):
        def body(i, carry):
            at = half_at(side, i)
            high, low = split(t_buf[at])
            wide = lax.dot_general(high, vcat[...], (((1,), (0,)), ((), ())), preferred_element_type=F32)
            rest = lax.dot_general(low, vcat[:, :size], (((1,), (0,)), ((), ())), preferred_element_type=F32)
            part[at] = wide[:, :size] + (wide[:, size:] + rest)

            @pl.when(side != h)
            def _():
                red_copy(i).start()

            return carry

        lax.fori_loop(0, per_half, body, 0)

    times(1 - h)
    times(h)

    small_rows = PAIR // 2 * chunk_rows
    tiles = half // small_rows
    last = bits - 1

    def small_at(i):
        return pl.ds(i * small_rows, small_rows)

    def side_at(side, i):
        return pl.ds(pl.multiple_of(side * half + i * small_rows, small_rows), small_rows)

    def bit_copy(bit, i):
        return remote(
            acc.at[bit, small_at(i)], got.at[bit, small_at(i)], bit_send.at[bit, i], bit_recv.at[bit, i],
            {"pcol": flip(bit)},
        )

    def back_copy(i, side):
        at = side_at(side, i)
        return remote(prod.at[at], prod.at[at], back_send.at[i], back_recv.at[i], mate)

    for i in range(per_half):
        red_copy(i).wait_recv()
        if bits > 1:
            acc[1, tile_of(i)] = part[half_at(h, i)] + got[0, tile_of(i)]
            for j in range(i * TILE // small_rows, (i + 1) * TILE // small_rows):
                bit_copy(1, j).start()

    def row_vectors(i, carry):
        at = tile_of(i)
        value = pair_dot(split(panel_ref[at]), linv_pair, ((1,), (1,))) + unit(me * rows + i * TILE)
        vec[at] = value
        left_hi[at, :size], left_lo[at, :size] = split(value)
        return carry

    lax.fori_loop(0, rows // TILE, row_vectors, 0)
    small_ref[...] = exact_dot(vec[...], part[...], ((0,), (0,)))
    sends = scatter(small_ref, rs2_ref, rs2_send, rs2_recv)
    for copy in sends:
        copy.start()

    for bit in range(1, last):
        for i in range(tiles):
            bit_copy(bit, i).wait_recv()
            acc[bit + 1, small_at(i)] = acc[bit, small_at(i)] + got[bit, small_at(i)]
            bit_copy(bit + 1, i).start()

    def across(offset):
        to = (q + offset) % m
        return remote(pc_ref.at[q], pc_ref.at[q], pc_send.at[offset], pc_recv.at[offset], {"pcol": to})

    def came(offset):
        slot = pc_ref.at[(q - offset + m) % m]
        return remote(slot, slot, pc_send.at[offset], pc_recv.at[offset], {"pcol": (q + offset) % m})

    crossing = [across(o) for o in range(1, m)]
    for i in range(tiles + 1):
        if i < tiles:
            if bits > 1:
                bit_copy(last, i).wait_recv()
                prod[side_at(h, i)] = acc[last, small_at(i)] + got[last, small_at(i)]
            else:
                prod[side_at(h, i)] = part[side_at(h, i)] + got[0, small_at(i)]
            back_copy(i, h).start()
        if i == tiles // 2:
            for copy in sends:
                copy.wait_recv()
            pc_ref[q] = collected(small_ref, rs2_ref)
            for copy in crossing:
                copy.start()
        if i > 0:
            back_copy(i - 1, 1 - h).wait_recv()
            for step in range(PAIR * (i - 1), PAIR * i):
                pump_q(step)
    fill(colq, prod)
    for o in range(1, m):
        came(o).wait_recv()
    value = pc_ref[0]
    for j in range(1, m):
        value = value + pc_ref[j]
    both2[me] = value
    sends2, arrivals = spread(both2, ag2_send, ag2_recv)
    for copy in sends2:
        copy.start()

    def rest(step, carry):
        pump_q(step)
        return carry

    lax.fori_loop(CHUNKS, total_steps, rest, 0)
    for copy in arrivals:
        copy.wait_recv()
    inner = exact_dot(both2[...].reshape(size, size), coupling, ((1,), (0,)))
    small = exact_dot(coupling, inner, ((0,), (0,)))
    coupling_pair = split(coupling)
    small_pair = split(-0.5 * small)

    def row_update(i, carry):
        at = tile_of(i)
        value = pair_dot(split(prod[at]), coupling_pair, ((1,), (0,)))
        value = value + pair_dot((left_hi[at, :size], left_lo[at, :size]), small_pair, ((1,), (0,)))
        left_hi[at, size:], left_lo[at, size:] = split(value)
        return carry

    lax.fori_loop(0, rows // TILE, row_update, 0)
    fill_wait(colq, prod)

    for j in range(tiles):
        settle(colq, pump2_send, pump2_recv, paired, range(PAIR * j, PAIR * (j + 1)))

        def col_update(i, carry):
            at = pl.ds(pl.multiple_of(i * half + j * small_rows, small_rows), small_rows)
            value = pair_dot(split(colq[at]), coupling_pair, ((1,), (0,)))
            value = value + pair_dot((vcat[at, :size], vcat[at, size:]), small_pair, ((1,), (0,)))
            right_hi[at, :size], right_lo[at, :size] = split(value)
            return carry

        lax.fori_loop(0, 2 * blocks, col_update, 0)
    for copy in crossing:
        copy.wait_send()
    for copy in sends + sends2:
        copy.wait_send()
    for i in range(per_half):
        red_copy(i).wait_send()
    for i in range(tiles):
        back_copy(i, h).wait_send()
        for bit in range(1, bits):
            bit_copy(bit, i).wait_send()
    drain(colp, pump_send, pump_recv)
    drain(colq, pump2_send, pump2_recv)


def exchange(panel, trailing, n, m, nx):
    rows, size = panel.shape
    cols = trailing.shape[1]
    blocks = cols // rows
    piece, half = size // n, rows // 2
    bits = max(m.bit_length() - 1, 2)
    tiles = half // (PAIR // 2 * (rows // CHUNKS))
    dma = pltpu.SemaphoreType.DMA
    vmem = pl.BlockSpec(memory_space=pltpu.VMEM)
    narrow = jnp.bfloat16
    return pl.pallas_call(
        functools.partial(exchange_kernel, (n, m, nx, blocks)),
        out_shape=[
            jax.ShapeDtypeStruct((rows, 2 * size), narrow),
            jax.ShapeDtypeStruct((rows, 2 * size), narrow),
            jax.ShapeDtypeStruct((cols, 2 * size), narrow),
            jax.ShapeDtypeStruct((cols, 2 * size), narrow),
            jax.ShapeDtypeStruct((size, size), F32),
            jax.ShapeDtypeStruct((rows, cols), F32),
        ],
        in_specs=[pl.BlockSpec(memory_space=pltpu.HBM)] * 2,
        out_specs=[vmem] * 6,
        scratch_shapes=[
            pltpu.VMEM((rows, size), F32),
            dma,
            dma,
            dma,
            pltpu.VMEM((cols, size), F32),
            pltpu.VMEM((cols, size), F32),
            pltpu.VMEM((cols, 2 * size), narrow),
            pltpu.VMEM((rows, size), F32),
            pltpu.VMEM((bits, half, size), F32),
            pltpu.VMEM((bits, half, size), F32),
            pltpu.VMEM((rows, size), F32),
            pltpu.VMEM((rows, size), F32),
            pltpu.VMEM((size, size), F32),
            pltpu.VMEM((n, piece, size), F32),
            pltpu.VMEM((n, 2, piece, size), F32),
            pltpu.VMEM((size, size), F32),
            pltpu.VMEM((n, piece, size), F32),
            pltpu.VMEM((m, piece, size), F32),
            pltpu.VMEM((n, piece, size), F32),
            dma((n,)), dma,
            dma((n,)), dma((n,)), dma((n,)), dma((n,)),
            dma((n,)), dma((n,)), dma((n,)), dma((n,)),
            dma((m,)), dma((m,)),
            dma((blocks, 4)), dma((blocks, CHUNKS)),
            dma((blocks, 4)), dma((blocks, CHUNKS)),
            dma((half // TILE,)), dma((half // TILE,)),
            dma((bits, tiles)), dma((bits, tiles)),
            dma((tiles,)), dma((tiles,)),
        ],
        compiler_params=pltpu.CompilerParams(
            collective_id=0, has_side_effects=True, vmem_limit_bytes=40 * 1024 * 1024
        ),
        name="exchange",
    )(panel, trailing)


def finish_kernel(t_ref, lh, ll, rh, rl, band_ref, out_ref, band_out):
    dims = (((1,), (1,)), ((), ()))
    wide = out_ref.shape[1]
    at = pl.ds(pl.multiple_of(pl.program_id(0) * wide, wide), wide)

    def one(a, b):
        return lax.dot_general(a, b, dims, preferred_element_type=F32)

    out_ref[...] = t_ref[:, at] - (
        one(lh[...], rh[at]) + (one(lh[...], rl[at]) + one(ll[...], rh[at]))
    )

    @pl.when(pl.program_id(0) == 0)
    def _():
        band_out[...] = band_ref[...]


def finish(trailing, lh, ll, rh, rl, band):
    rows, cols = trailing.shape
    tile = 2 * TILE
    whole = pl.BlockSpec(memory_space=pltpu.VMEM)
    return pl.pallas_call(
        finish_kernel,
        grid=(cols // tile,),
        out_shape=[jax.ShapeDtypeStruct((rows, cols), F32), jax.ShapeDtypeStruct(band.shape, F32)],
        in_specs=[whole] * 6,
        out_specs=[pl.BlockSpec((rows, tile), lambda i: (0, i)), whole],
        compiler_params=pltpu.CompilerParams(vmem_limit_bytes=GRANT),
        name="finish",
    )(trailing, lh, ll, rh, rl, band)


def shards(n, m, nx, panel, trailing):
    lh, ll, rh, rl, band, held = exchange(panel, trailing, n, m, nx)
    return tuple(finish(held, lh, ll, rh, rl, band))


def solution(mesh):
    placed = (P("prow", None), P("prow", "pcol"))
    n, m = mesh.shape["prow"], mesh.shape["pcol"]
    column = [getattr(d, "coords", None) for d in mesh.devices[:, 0]]
    nx = 2 if None in column else len({c[0] for c in column})
    return jax.shard_map(
        functools.partial(shards, n, m, nx),
        mesh=mesh,
        in_specs=placed,
        out_specs=(P("prow", "pcol"), P()),
        check_vma=False,
    )
```

```python
import functools

import jax
import jax.numpy as jnp
from jax import lax
from jax.experimental import pallas as pl
from jax.experimental.pallas import tpu as pltpu
from jax.sharding import PartitionSpec as P

STEPS = 16


def factor_body(gram, top_t, between):
    size = gram.shape[0]
    rows = lax.broadcasted_iota(jnp.int32, (size, size), 0)
    cols = lax.broadcasted_iota(jnp.int32, (size, size), 1)

    def block(turn, carry):
        work, other = carry
        live = size - turn * STEPS
        for k in range(STEPS):
            if k % (STEPS // 2) == 0:
                between(2 * turn + 2 * k // STEPS)
            at_col = cols == k
            below = jnp.logical_and(rows > k, rows < live)
            col = jnp.broadcast_to(work[:, k : k + 1], (size, size))
            row_scale = lax.rsqrt(col[k : k + 1, :])
            row = jnp.where(at_col[:1], 1.0, work[k : k + 1, :]) * row_scale
            low = jnp.where(jnp.logical_and(rows >= k, rows < live), col * row_scale, 0.0)
            work = jnp.where(
                rows == k,
                row,
                jnp.where(below, jnp.where(at_col, 0.0, work) - low * row, work),
            )
            ocol = jnp.broadcast_to(other[:, k : k + 1], (size, size)) + low
            inv = 1.0 / ocol[k : k + 1, :]
            orow = jnp.where(at_col[:1], 1.0, other[k : k + 1, :]) * inv
            other = jnp.where(
                rows == k, orow, jnp.where(at_col, 0.0, other) - ocol * orow
            )
        work = jnp.concatenate([work[STEPS:], work[:STEPS]], axis=0)
        other = jnp.concatenate([other[STEPS:], other[:STEPS]], axis=0)
        return pltpu.roll(work, size - STEPS, 1), pltpu.roll(other, size - STEPS, 1)

    return lax.fori_loop(0, size // STEPS, block, (gram, top_t))


def split_factor(work, other):
    size = work.shape[0]
    rows = lax.broadcasted_iota(jnp.int32, (size, size), 0)
    cols = lax.broadcasted_iota(jnp.int32, (size, size), 1)
    linv = jnp.where(rows >= cols, work, 0.0)
    upper = jnp.where(rows < cols, work, jnp.where(rows == cols, 1.0 / jnp.where(rows == cols, work, 1.0), 0.0))
    coupling = lax.dot_general(
        other, upper, (((1,), (1,)), ((), ())), precision=lax.Precision.HIGHEST, preferred_element_type=jnp.float32
    )
    return linv, upper, coupling

MESH = pl.DeviceIdType.MESH
CHUNKS = 16
EARLY = (4, 4, 4)
SLACK = (4, 4)
TILE = 256
PAIR = 4
GRANT = 24 * 1024 * 1024
F32 = jnp.float32


def exact_dot(left, right, dims):
    return lax.dot_general(
        left, right, (dims, ((), ())), precision=lax.Precision.HIGHEST, preferred_element_type=F32
    )


def split(value):
    high = value.astype(jnp.bfloat16)
    return high, (value - high.astype(F32)).astype(jnp.bfloat16)


def pair_dot(left, right, dims):
    (lh, ll), (rh, rl) = left, right

    def one(a, b):
        return lax.dot_general(a, b, (dims, ((), ())), preferred_element_type=F32)

    return one(lh, rh) + (one(lh, rl) + one(ll, rh))


def exchange_kernel(
    sizes, panel_ref, trail_ref, left_hi, left_lo, right_hi, right_lo, band_ref, t_buf,
    own_sem, t_sem, colp, colq, vcat, part, acc, got, prod, vec,
    gram_ref, rs_ref, both, small_ref, rs2_ref, pc_ref, both2,
    top_send, top_recv, rs_send, rs_recv, ag_send, ag_recv, rs2_send, rs2_recv, ag2_send, ag2_recv, pc_send, pc_recv,
    pump_send, pump_recv, pump2_send, pump2_recv, red_send, red_recv, bit_send, bit_recv, back_send, back_recv,
):
    n, m, nx, blocks = sizes
    nz = n // nx
    rows, size = panel_ref.shape
    piece = size // n
    half = rows // 2
    chunk_rows = rows // CHUNKS
    me = lax.axis_index("prow")
    q = lax.axis_index("pcol")
    z, x = me // nx, me % nx
    bits = m.bit_length() - 1

    def flip(bit):
        step = 1 << bit
        return q + step - 2 * step * ((q // step) % 2)

    def peer(offset):
        return (me + offset) % n

    def remote(src, dst, send, recv, where):
        return pltpu.make_async_remote_copy(
            src_ref=src, dst_ref=dst, send_sem=send, recv_sem=recv, device_id=where, device_id_type=MESH
        )

    t_copy = pltpu.make_async_copy(trail_ref, t_buf, t_sem)
    t_copy.start()
    barrier = pltpu.get_barrier_semaphore()
    for offset in range(1, n):
        pl.semaphore_signal(barrier, inc=1, device_id={"prow": peer(offset)}, device_id_type=MESH)
    for offset in range(1, m):
        pl.semaphore_signal(barrier, inc=1, device_id={"pcol": (q + offset) % m}, device_id_type=MESH)

    def place(k):
        b = q * blocks + k
        return b, z - b // nx, x - b % nx

    def filled(buf, source):
        copies = []
        for k in range(blocks):
            b, _, _ = place(k)
            copies.append((me == b, pltpu.make_async_copy(source, buf.at[pl.ds(k * rows, rows)], own_sem)))
        return copies

    def fill(buf, source):
        for mine, copy in filled(buf, source):
            pl.when(mine)(copy.start)

    def fill_wait(buf, source):
        for mine, copy in filled(buf, source):
            pl.when(mine)(copy.wait)

    fill(colp, panel_ref)
    gram_ref[...] = exact_dot(panel_ref[...], panel_ref[...], ((0,), (0,)))
    fill_wait(colp, panel_ref)
    pl.semaphore_wait(barrier, n - 1 + m - 1)

    def children(dz, dx):
        return (
            (jnp.logical_and(jnp.logical_and(dx == 0, dz >= 0), z < nz - 1), me + nx),
            (jnp.logical_and(jnp.logical_and(dx == 0, dz <= 0), z > 0), me - nx),
            (jnp.logical_and(dx >= 0, x < nx - 1), me + 1),
            (jnp.logical_and(dx <= 0, x > 0), me - 1),
        )

    def relays(dz, dx):
        flags = [has for has, _ in children(dz, dx)]
        return functools.reduce(jnp.logical_or, flags)

    def in_order(k, c):
        return pl.multiple_of(c * chunk_rows, chunk_rows)

    def paired(k, c):
        first = place(k)[0] // blocks % 2
        side = (first + c % PAIR // (PAIR // 2)) % 2
        at = side * half + c // PAIR * (PAIR // 2) * chunk_rows + c % (PAIR // 2) * chunk_rows
        return pl.multiple_of(at, chunk_rows)

    def settle(buf, send, recv, where, span):
        for k in range(blocks):
            _, dz, dx = place(k)
            away = jnp.logical_or(dz != 0, dx != 0)

            @pl.when(jnp.logical_and(away, jnp.logical_not(relays(dz, dx))))
            def _():
                for c in span:
                    part_of = buf.at[pl.ds(k * rows + where(k, c), chunk_rows)]
                    remote(part_of, part_of, send.at[k, 0], recv.at[k, c], {"prow": peer(1)}).wait_recv()

    def pump(step, buf, source, send, recv, where, slack):
        for k in range(blocks):
            _, dz, dx = place(k)
            far = jnp.where(dz < 0, -dz, dz) + jnp.where(dx < 0, -dx, dx)
            c = step - slack * far

            @pl.when(jnp.logical_and(c >= 0, c < CHUNKS))
            def _():
                part_of = buf.at[pl.ds(k * rows + where(k, c), chunk_rows)]

                @pl.when(jnp.logical_and(far > 0, relays(dz, dx)))
                def _():
                    remote(part_of, part_of, send.at[k, 0], recv.at[k, c], {"prow": peer(1)}).wait_recv()

                for d, (has, to) in enumerate(children(dz, dx)):

                    @pl.when(jnp.logical_and(has, far > 0))
                    def _():
                        remote(part_of, part_of, send.at[k, d], recv.at[k, c], {"prow": to}).start()

                    @pl.when(jnp.logical_and(has, far == 0))
                    def _():
                        own = source.at[pl.ds(where(k, c), chunk_rows)]
                        remote(own, part_of, send.at[k, d], recv.at[k, c], {"prow": to}).start()

    def pump_p(step):
        pump(step, colp, panel_ref, pump_send, pump_recv, in_order, SLACK[0])

    def pump_q(step):
        pump(step, colq, prod, pump2_send, pump2_recv, paired, SLACK[1])

    def drain(buf, send, recv):
        for k in range(blocks):
            _, dz, dx = place(k)
            whole = buf.at[pl.ds(k * rows, rows)]
            for d, (has, to) in enumerate(children(dz, dx)):

                @pl.when(has)
                def _():
                    remote(whole, whole, send.at[k, d], recv.at[k, 0], {"prow": peer(1)}).wait_send()

    steps_p, steps_q = [CHUNKS + slack * (nz - 1 + max(nx - 1, 0)) for slack in SLACK]

    def scatter(src, slots, send, recv):
        def copy(offset):
            to = peer(offset)
            return remote(
                src.at[pl.ds(to * piece, piece)], slots.at[offset], send.at[offset], recv.at[offset], {"prow": to}
            )

        return [copy(offset) for offset in range(1, n)]

    def spread(slots, send, recv):
        def copy(offset):
            return remote(slots.at[me], slots.at[me], send.at[offset], recv.at[offset], {"prow": peer(offset)})

        def arrive(offset):
            slot = slots.at[peer(n - offset)]
            return remote(slot, slot, send.at[offset], recv.at[offset], {"prow": peer(offset)})

        return [copy(o) for o in range(1, n)], [arrive(o) for o in range(1, n)]

    def collected(src, slots):
        value = src[pl.ds(me * piece, piece)]
        for offset in range(1, n):
            value = value + slots[offset]
        return value

    def top_copy(j):
        return remote(panel_ref.at[pl.ds(j * piece, piece)], both.at[j, 1], top_send.at[j], top_recv, {"prow": j})

    @pl.when(me == 0)
    def _():
        for j in range(1, n):
            top_copy(j).start()
        both[0, 1] = panel_ref[:piece]

    for step in range(EARLY[0]):
        pump_p(step)
    sends = scatter(gram_ref, rs_ref, rs_send, rs_recv)
    for copy in sends:
        copy.start()
    for step in range(EARLY[0], sum(EARLY[:2])):
        pump_p(step)

    @pl.when(me > 0)
    def _():
        slot = both.at[me, 1]
        remote(slot, slot, top_send.at[0], top_recv, {"prow": peer(1)}).wait_recv()

    for copy in sends:
        copy.wait_recv()
    both[me, 0] = collected(gram_ref, rs_ref)
    sends2, arrivals = spread(both, ag_send, ag_recv)
    for copy in sends2:
        copy.start()
    for step in range(sum(EARLY[:2]), sum(EARLY)):
        pump_p(step)
    for copy in arrivals:
        copy.wait_recv()
    for copy in sends + sends2:
        copy.wait_send()

    @pl.when(me == 0)
    def _():
        for j in range(1, n):
            top_copy(j).wait_send()

    done = sum(EARLY)
    turns = 2 * (size // STEPS)
    work, other = factor_body(
        both[:, 0].reshape(size, size),
        both[:, 1].reshape(size, size).T,
        lambda turn: pump_p(done + turn),
    )
    for step in range(done + turns, steps_p):
        pump_p(step)
    settle(colp, pump_send, pump_recv, in_order, range(CHUNKS))
    linv, upper, coupling = split_factor(work, other)
    band_ref[...] = -upper
    linv_pair = split(linv)
    coupling_pair = split(coupling)

    def unit(start):
        r = lax.broadcasted_iota(jnp.int32, (TILE, size), 0) + start
        return jnp.where(r == lax.broadcasted_iota(jnp.int32, (TILE, size), 1), 1.0, 0.0)

    def col_vectors(i, carry):
        at = pl.ds(pl.multiple_of(i * TILE, TILE), TILE)
        value = pair_dot(split(colp[at]), linv_pair, ((1,), (1,))) + unit(q * blocks * rows + i * TILE)
        high, low = split(value)
        vcat[at, :size] = high
        vcat[at, size:] = low
        right_hi[at, size:] = high
        right_lo[at, size:] = low
        return carry

    lax.fori_loop(0, blocks * rows // TILE, col_vectors, 0)
    t_copy.wait()

    h = q % 2
    per_half = half // TILE
    mate = {"pcol": flip(0)}

    def half_at(side, i):
        return pl.ds(pl.multiple_of(side * half + i * TILE, TILE), TILE)

    def tile_of(i):
        return pl.ds(pl.multiple_of(i * TILE, TILE), TILE)

    def red_copy(i):
        return remote(part.at[half_at(1 - h, i)], got.at[0, tile_of(i)], red_send.at[i], red_recv.at[i], mate)

    def times(side):
        def body(i, carry):
            at = half_at(side, i)
            high, low = split(t_buf[at])
            wide = lax.dot_general(high, vcat[...], (((1,), (0,)), ((), ())), preferred_element_type=F32)
            rest = lax.dot_general(low, vcat[:, :size], (((1,), (0,)), ((), ())), preferred_element_type=F32)
            part[at] = wide[:, :size] + (wide[:, size:] + rest)

            @pl.when(side != h)
            def _():
                red_copy(i).start()

            return carry

        lax.fori_loop(0, per_half, body, 0)

    times(1 - h)
    times(h)

    small_rows = PAIR // 2 * chunk_rows
    tiles = half // small_rows
    last = bits - 1

    def small_at(i):
        return pl.ds(i * small_rows, small_rows)

    def side_at(side, i):
        return pl.ds(pl.multiple_of(side * half + i * small_rows, small_rows), small_rows)

    def bit_copy(bit, i):
        return remote(
            acc.at[bit, small_at(i)], got.at[bit, small_at(i)], bit_send.at[bit, i], bit_recv.at[bit, i],
            {"pcol": flip(bit)},
        )

    def back_copy(i, side):
        at = side_at(side, i)
        return remote(prod.at[at], prod.at[at], back_send.at[i], back_recv.at[i], mate)

    for i in range(per_half):
        red_copy(i).wait_recv()
        if bits > 1:
            acc[1, tile_of(i)] = part[half_at(h, i)] + got[0, tile_of(i)]
            for j in range(i * TILE // small_rows, (i + 1) * TILE // small_rows):
                bit_copy(1, j).start()

    def row_vectors(i, carry):
        at = tile_of(i)
        value = pair_dot(split(panel_ref[at]), linv_pair, ((1,), (1,))) + unit(me * rows + i * TILE)
        vec[at] = value
        left_hi[at, :size], left_lo[at, :size] = split(value)
        return carry

    lax.fori_loop(0, rows // TILE, row_vectors, 0)
    small_ref[...] = exact_dot(vec[...], part[...], ((0,), (0,)))
    sends = scatter(small_ref, rs2_ref, rs2_send, rs2_recv)
    for copy in sends:
        copy.start()

    for bit in range(1, last):
        for i in range(tiles):
            bit_copy(bit, i).wait_recv()
            acc[bit + 1, small_at(i)] = acc[bit, small_at(i)] + got[bit, small_at(i)]
            bit_copy(bit + 1, i).start()

    def across(offset):
        to = (q + offset) % m
        return remote(pc_ref.at[q], pc_ref.at[q], pc_send.at[offset], pc_recv.at[offset], {"pcol": to})

    def came(offset):
        slot = pc_ref.at[(q - offset + m) % m]
        return remote(slot, slot, pc_send.at[offset], pc_recv.at[offset], {"pcol": (q + offset) % m})

    crossing = [across(o) for o in range(1, m)]
    for i in range(tiles + 1):
        if i < tiles:
            if bits > 1:
                bit_copy(last, i).wait_recv()
                value = acc[last, small_at(i)] + got[last, small_at(i)]
            else:
                value = part[side_at(h, i)] + got[0, small_at(i)]
            prod[side_at(h, i)] = pair_dot(split(value), coupling_pair, ((1,), (0,)))
            back_copy(i, h).start()
        if i == tiles // 2:
            for copy in sends:
                copy.wait_recv()
            pc_ref[q] = collected(small_ref, rs2_ref)
            for copy in crossing:
                copy.start()
        if i > 0:
            back_copy(i - 1, 1 - h).wait_recv()
            for step in range(PAIR * (i - 1), PAIR * i):
                pump_q(step)
    fill(colq, prod)
    for o in range(1, m):
        came(o).wait_recv()
    value = pc_ref[0]
    for j in range(1, m):
        value = value + pc_ref[j]
    both2[me] = value
    sends2, arrivals = spread(both2, ag2_send, ag2_recv)
    for copy in sends2:
        copy.start()

    def rest(step, carry):
        pump_q(step)
        return carry

    lax.fori_loop(CHUNKS, steps_q, rest, 0)
    for copy in arrivals:
        copy.wait_recv()
    inner = exact_dot(both2[...].reshape(size, size), coupling, ((1,), (0,)))
    small = exact_dot(coupling, inner, ((0,), (0,)))
    small_pair = split(small)

    def row_update(i, carry):
        at = tile_of(i)
        value = prod[at] - pair_dot((left_hi[at, :size], left_lo[at, :size]), small_pair, ((1,), (0,)))
        left_hi[at, size:], left_lo[at, size:] = split(value)
        return carry

    lax.fori_loop(0, rows // TILE, row_update, 0)
    fill_wait(colq, prod)

    for j in range(tiles):
        settle(colq, pump2_send, pump2_recv, paired, range(PAIR * j, PAIR * (j + 1)))

        def col_update(i, carry):
            at = pl.ds(pl.multiple_of(i * half + j * small_rows, small_rows), small_rows)
            right_hi[at, :size], right_lo[at, :size] = split(colq[at])
            return carry

        lax.fori_loop(0, 2 * blocks, col_update, 0)
    for copy in crossing:
        copy.wait_send()
    for copy in sends + sends2:
        copy.wait_send()
    for i in range(per_half):
        red_copy(i).wait_send()
    for i in range(tiles):
        back_copy(i, h).wait_send()
        for bit in range(1, bits):
            bit_copy(bit, i).wait_send()
    drain(colp, pump_send, pump_recv)
    drain(colq, pump2_send, pump2_recv)


def exchange(panel, trailing, n, m, nx):
    rows, size = panel.shape
    cols = trailing.shape[1]
    blocks = cols // rows
    piece, half = size // n, rows // 2
    bits = max(m.bit_length() - 1, 2)
    tiles = half // (PAIR // 2 * (rows // CHUNKS))
    dma = pltpu.SemaphoreType.DMA
    vmem = pl.BlockSpec(memory_space=pltpu.VMEM)
    narrow = jnp.bfloat16
    return pl.pallas_call(
        functools.partial(exchange_kernel, (n, m, nx, blocks)),
        out_shape=[
            jax.ShapeDtypeStruct((rows, 2 * size), narrow),
            jax.ShapeDtypeStruct((rows, 2 * size), narrow),
            jax.ShapeDtypeStruct((cols, 2 * size), narrow),
            jax.ShapeDtypeStruct((cols, 2 * size), narrow),
            jax.ShapeDtypeStruct((size, size), F32),
            jax.ShapeDtypeStruct((rows, cols), F32),
        ],
        in_specs=[vmem, pl.BlockSpec(memory_space=pltpu.HBM)],
        out_specs=[vmem] * 6,
        scratch_shapes=[
            dma,
            dma,
            pltpu.VMEM((cols, size), F32),
            pltpu.VMEM((cols, size), F32),
            pltpu.VMEM((cols, 2 * size), narrow),
            pltpu.VMEM((rows, size), F32),
            pltpu.VMEM((bits, half, size), F32),
            pltpu.VMEM((bits, half, size), F32),
            pltpu.VMEM((rows, size), F32),
            pltpu.VMEM((rows, size), F32),
            pltpu.VMEM((size, size), F32),
            pltpu.VMEM((n, piece, size), F32),
            pltpu.VMEM((n, 2, piece, size), F32),
            pltpu.VMEM((size, size), F32),
            pltpu.VMEM((n, piece, size), F32),
            pltpu.VMEM((m, piece, size), F32),
            pltpu.VMEM((n, piece, size), F32),
            dma((n,)), dma,
            dma((n,)), dma((n,)), dma((n,)), dma((n,)),
            dma((n,)), dma((n,)), dma((n,)), dma((n,)),
            dma((m,)), dma((m,)),
            dma((blocks, 4)), dma((blocks, CHUNKS)),
            dma((blocks, 4)), dma((blocks, CHUNKS)),
            dma((half // TILE,)), dma((half // TILE,)),
            dma((bits, tiles)), dma((bits, tiles)),
            dma((tiles,)), dma((tiles,)),
        ],
        compiler_params=pltpu.CompilerParams(
            collective_id=0, has_side_effects=True, vmem_limit_bytes=40 * 1024 * 1024
        ),
        name="exchange",
    )(panel, trailing)


def finish_kernel(t_ref, lh, ll, rh, rl, band_ref, out_ref, band_out):
    dims = (((1,), (1,)), ((), ()))
    wide = out_ref.shape[1]
    at = pl.ds(pl.multiple_of(pl.program_id(0) * wide, wide), wide)

    def one(a, b):
        return lax.dot_general(a, b, dims, preferred_element_type=F32)

    out_ref[...] = t_ref[:, at] - (
        one(lh[...], rh[at]) + (one(lh[...], rl[at]) + one(ll[...], rh[at]))
    )

    @pl.when(pl.program_id(0) == 0)
    def _():
        band_out[...] = band_ref[...]


def finish(trailing, lh, ll, rh, rl, band):
    rows, cols = trailing.shape
    tile = 2 * TILE
    whole = pl.BlockSpec(memory_space=pltpu.VMEM)
    return pl.pallas_call(
        finish_kernel,
        grid=(cols // tile,),
        out_shape=[jax.ShapeDtypeStruct((rows, cols), F32), jax.ShapeDtypeStruct(band.shape, F32)],
        in_specs=[whole] * 6,
        out_specs=[pl.BlockSpec((rows, tile), lambda i: (0, i)), whole],
        compiler_params=pltpu.CompilerParams(vmem_limit_bytes=GRANT),
        name="finish",
    )(trailing, lh, ll, rh, rl, band)


def shards(n, m, nx, panel, trailing):
    lh, ll, rh, rl, band, held = exchange(panel, trailing, n, m, nx)
    return tuple(finish(held, lh, ll, rh, rl, band))


def solution(mesh):
    placed = (P("prow", None), P("prow", "pcol"))
    n, m = mesh.shape["prow"], mesh.shape["pcol"]
    column = [getattr(d, "coords", None) for d in mesh.devices[:, 0]]
    nx = 2 if None in column else len({c[0] for c in column})
    return jax.shard_map(
        functools.partial(shards, n, m, nx),
        mesh=mesh,
        in_specs=placed,
        out_specs=(P("prow", "pcol"), P()),
        check_vma=False,
    )
```

```python
import functools

import jax
import jax.numpy as jnp
from jax import lax
from jax.experimental import pallas as pl
from jax.experimental.pallas import tpu as pltpu
from jax.sharding import PartitionSpec as P

STEPS = 16


def factor_body(gram, top_t, between):
    size = gram.shape[0]
    rows = lax.broadcasted_iota(jnp.int32, (size, size), 0)
    cols = lax.broadcasted_iota(jnp.int32, (size, size), 1)

    def block(turn, carry):
        work, other = carry
        live = size - turn * STEPS
        for k in range(STEPS):
            if k % (STEPS // 2) == 0:
                between(2 * turn + 2 * k // STEPS)
            at_col = cols == k
            below = jnp.logical_and(rows > k, rows < live)
            col = jnp.broadcast_to(work[:, k : k + 1], (size, size))
            row_scale = lax.rsqrt(col[k : k + 1, :])
            row = jnp.where(at_col[:1], 1.0, work[k : k + 1, :]) * row_scale
            low = jnp.where(jnp.logical_and(rows >= k, rows < live), col * row_scale, 0.0)
            work = jnp.where(
                rows == k,
                row,
                jnp.where(below, jnp.where(at_col, 0.0, work) - low * row, work),
            )
            ocol = jnp.broadcast_to(other[:, k : k + 1], (size, size)) + low
            inv = 1.0 / ocol[k : k + 1, :]
            orow = jnp.where(at_col[:1], 1.0, other[k : k + 1, :]) * inv
            other = jnp.where(
                rows == k, orow, jnp.where(at_col, 0.0, other) - ocol * orow
            )
        work = jnp.concatenate([work[STEPS:], work[:STEPS]], axis=0)
        other = jnp.concatenate([other[STEPS:], other[:STEPS]], axis=0)
        return pltpu.roll(work, size - STEPS, 1), pltpu.roll(other, size - STEPS, 1)

    return lax.fori_loop(0, size // STEPS, block, (gram, top_t))


def split_factor(work, other):
    size = work.shape[0]
    rows = lax.broadcasted_iota(jnp.int32, (size, size), 0)
    cols = lax.broadcasted_iota(jnp.int32, (size, size), 1)
    linv = jnp.where(rows >= cols, work, 0.0)
    upper = jnp.where(rows < cols, work, jnp.where(rows == cols, 1.0 / jnp.where(rows == cols, work, 1.0), 0.0))
    coupling = lax.dot_general(
        other, upper, (((1,), (1,)), ((), ())), precision=lax.Precision.HIGHEST, preferred_element_type=jnp.float32
    )
    return linv, upper, coupling

MESH = pl.DeviceIdType.MESH
CHUNKS = 16
EARLY = (1, 4, 4)
SLACK = (4, 4)
TILE = 256
PIECE = 64
PAIR = 4
GRANT = 24 * 1024 * 1024
F32 = jnp.float32


def exact_dot(left, right, dims):
    return lax.dot_general(
        left, right, (dims, ((), ())), precision=lax.Precision.HIGHEST, preferred_element_type=F32
    )


def split(value):
    high = value.astype(jnp.bfloat16)
    return high, (value - high.astype(F32)).astype(jnp.bfloat16)


def pair_dot(left, right, dims):
    (lh, ll), (rh, rl) = left, right

    def one(a, b):
        return lax.dot_general(a, b, (dims, ((), ())), preferred_element_type=F32)

    return one(lh, rh) + (one(lh, rl) + one(ll, rh))


def exchange_kernel(
    sizes, panel_ref, trail_ref, left_hi, left_lo, right_hi, right_lo, band_ref, t_buf,
    own_sem, t_sem, colp, colq, vcat, t_hi, t_lo, part, acc, got, prod, vec,
    gram_ref, rs_ref, both, small_ref, rs2_ref, pc_ref, both2,
    top_send, top_recv, rs_send, rs_recv, ag_send, ag_recv, rs2_send, rs2_recv, ag2_send, ag2_recv, pc_send, pc_recv,
    pump_send, pump_recv, pump2_send, pump2_recv, red_send, red_recv, bit_send, bit_recv, back_send, back_recv,
):
    n, m, nx, blocks = sizes
    nz = n // nx
    rows, size = panel_ref.shape
    piece = size // n
    half = rows // 2
    chunk_rows = rows // CHUNKS
    me = lax.axis_index("prow")
    q = lax.axis_index("pcol")
    z, x = me // nx, me % nx
    bits = m.bit_length() - 1

    def flip(bit):
        step = 1 << bit
        return q + step - 2 * step * ((q // step) % 2)

    def peer(offset):
        return (me + offset) % n

    def remote(src, dst, send, recv, where):
        return pltpu.make_async_remote_copy(
            src_ref=src, dst_ref=dst, send_sem=send, recv_sem=recv, device_id=where, device_id_type=MESH
        )

    t_copy = pltpu.make_async_copy(trail_ref, t_buf, t_sem)
    t_copy.start()
    barrier = pltpu.get_barrier_semaphore()
    for offset in range(1, n):
        pl.semaphore_signal(barrier, inc=1, device_id={"prow": peer(offset)}, device_id_type=MESH)
    for offset in range(1, m):
        pl.semaphore_signal(barrier, inc=1, device_id={"pcol": (q + offset) % m}, device_id_type=MESH)

    def place(k):
        b = q * blocks + k
        return b, z - b // nx, x - b % nx

    def filled(buf, source):
        copies = []
        for k in range(blocks):
            b, _, _ = place(k)
            copies.append((me == b, pltpu.make_async_copy(source, buf.at[pl.ds(k * rows, rows)], own_sem)))
        return copies

    def fill(buf, source):
        for mine, copy in filled(buf, source):
            pl.when(mine)(copy.start)

    def fill_wait(buf, source):
        for mine, copy in filled(buf, source):
            pl.when(mine)(copy.wait)

    fill(colp, panel_ref)
    gram_ref[...] = exact_dot(panel_ref[...], panel_ref[...], ((0,), (0,)))
    fill_wait(colp, panel_ref)
    pl.semaphore_wait(barrier, n - 1 + m - 1)

    def children(dz, dx):
        return (
            (jnp.logical_and(jnp.logical_and(dx == 0, dz >= 0), z < nz - 1), me + nx),
            (jnp.logical_and(jnp.logical_and(dx == 0, dz <= 0), z > 0), me - nx),
            (jnp.logical_and(dx >= 0, x < nx - 1), me + 1),
            (jnp.logical_and(dx <= 0, x > 0), me - 1),
        )

    def relays(dz, dx):
        flags = [has for has, _ in children(dz, dx)]
        return functools.reduce(jnp.logical_or, flags)

    def in_order(k, c):
        return pl.multiple_of(c * chunk_rows, chunk_rows)

    def paired(k, c):
        first = place(k)[0] // blocks % 2
        side = (first + c % PAIR // (PAIR // 2)) % 2
        at = side * half + c // PAIR * (PAIR // 2) * chunk_rows + c % (PAIR // 2) * chunk_rows
        return pl.multiple_of(at, chunk_rows)

    def settle(buf, send, recv, where, span):
        for k in range(blocks):
            _, dz, dx = place(k)
            away = jnp.logical_or(dz != 0, dx != 0)

            @pl.when(jnp.logical_and(away, jnp.logical_not(relays(dz, dx))))
            def _():
                for c in span:
                    part_of = buf.at[pl.ds(k * rows + where(k, c), chunk_rows)]
                    remote(part_of, part_of, send.at[k, 0], recv.at[k, c], {"prow": peer(1)}).wait_recv()

    def pump(step, buf, source, send, recv, where, slack):
        for k in range(blocks):
            _, dz, dx = place(k)
            far = jnp.where(dz < 0, -dz, dz) + jnp.where(dx < 0, -dx, dx)
            c = step - slack * far

            @pl.when(jnp.logical_and(relays(dz, dx), jnp.logical_and(c >= 0, c < CHUNKS)))
            def _():
                part_of = buf.at[pl.ds(k * rows + where(k, c), chunk_rows)]

                @pl.when(far > 0)
                def _():
                    remote(part_of, part_of, send.at[k, 0], recv.at[k, c], {"prow": peer(1)}).wait_recv()

                for d, (has, to) in enumerate(children(dz, dx)):

                    @pl.when(has if source is None else jnp.logical_and(has, far > 0))
                    def _():
                        remote(part_of, part_of, send.at[k, d], recv.at[k, c], {"prow": to}).start()

                    if source is not None:

                        @pl.when(jnp.logical_and(has, far == 0))
                        def _():
                            own = source.at[pl.ds(where(k, c), chunk_rows)]
                            remote(own, part_of, send.at[k, d], recv.at[k, c], {"prow": to}).start()

    def pump_p(step):
        pump(step, colp, None, pump_send, pump_recv, in_order, SLACK[0])

    def pump_q(step):
        pump(step, colq, prod, pump2_send, pump2_recv, paired, SLACK[1])

    def drain(buf, send, recv):
        for k in range(blocks):
            _, dz, dx = place(k)
            whole = buf.at[pl.ds(k * rows, rows)]
            for d, (has, to) in enumerate(children(dz, dx)):

                @pl.when(has)
                def _():
                    remote(whole, whole, send.at[k, d], recv.at[k, 0], {"prow": peer(1)}).wait_send()

    steps_p, steps_q = [CHUNKS + slack * (nz - 1 + max(nx - 2, 0)) for slack in SLACK]

    def scatter(src, slots, send, recv):
        def copy(offset):
            to = peer(offset)
            return remote(
                src.at[pl.ds(to * piece, piece)], slots.at[offset], send.at[offset], recv.at[offset], {"prow": to}
            )

        return [copy(offset) for offset in range(1, n)]

    def spread(slots, send, recv):
        def copy(offset):
            return remote(slots.at[me], slots.at[me], send.at[offset], recv.at[offset], {"prow": peer(offset)})

        def arrive(offset):
            slot = slots.at[peer(n - offset)]
            return remote(slot, slot, send.at[offset], recv.at[offset], {"prow": peer(offset)})

        return [copy(o) for o in range(1, n)], [arrive(o) for o in range(1, n)]

    def collected(src, slots):
        value = src[pl.ds(me * piece, piece)]
        for offset in range(1, n):
            value = value + slots[offset]
        return value

    def split_rows(side):
        def body(i, carry):
            at = pl.ds(pl.multiple_of(side * half + i * PIECE, PIECE), PIECE)
            t_hi[at], t_lo[at] = split(t_buf[at])
            return carry

        lax.fori_loop(0, half // PIECE, body, 0)

    def top_copy(j):
        return remote(panel_ref.at[pl.ds(j * piece, piece)], both.at[j, 1], top_send.at[j], top_recv, {"prow": j})

    @pl.when(me == 0)
    def _():
        for j in range(1, n):
            top_copy(j).start()
        both[0, 1] = panel_ref[:piece]

    for step in range(EARLY[0]):
        pump_p(step)
    sends = scatter(gram_ref, rs_ref, rs_send, rs_recv)
    for copy in sends:
        copy.start()
    for step in range(EARLY[0], sum(EARLY[:2])):
        pump_p(step)
    t_copy.wait()
    split_rows(0)

    @pl.when(me > 0)
    def _():
        slot = both.at[me, 1]
        remote(slot, slot, top_send.at[0], top_recv, {"prow": peer(1)}).wait_recv()

    for copy in sends:
        copy.wait_recv()
    both[me, 0] = collected(gram_ref, rs_ref)
    sends2, arrivals = spread(both, ag_send, ag_recv)
    for copy in sends2:
        copy.start()
    for step in range(sum(EARLY[:2]), sum(EARLY)):
        pump_p(step)
    split_rows(1)
    for copy in arrivals:
        copy.wait_recv()
    for copy in sends + sends2:
        copy.wait_send()

    @pl.when(me == 0)
    def _():
        for j in range(1, n):
            top_copy(j).wait_send()

    done = sum(EARLY)
    turns = 2 * (size // STEPS)
    work, other = factor_body(
        both[:, 0].reshape(size, size),
        both[:, 1].reshape(size, size).T,
        lambda turn: pump_p(done + turn),
    )
    for step in range(done + turns, steps_p):
        pump_p(step)
    settle(colp, pump_send, pump_recv, in_order, range(CHUNKS))
    linv, upper, coupling = split_factor(work, other)
    band_ref[...] = -upper
    linv_pair = split(linv)
    coupling_pair = split(coupling)

    def unit(start):
        r = lax.broadcasted_iota(jnp.int32, (TILE, size), 0) + start
        return jnp.where(r == lax.broadcasted_iota(jnp.int32, (TILE, size), 1), 1.0, 0.0)

    def col_vectors(i, carry):
        at = pl.ds(pl.multiple_of(i * TILE, TILE), TILE)
        value = pair_dot(split(colp[at]), linv_pair, ((1,), (1,))) + unit(q * blocks * rows + i * TILE)
        high, low = split(value)
        vcat[at, :size] = high
        vcat[at, size:] = low
        right_hi[at, size:] = high
        right_lo[at, size:] = low
        return carry

    lax.fori_loop(0, blocks * rows // TILE, col_vectors, 0)

    h = q % 2
    per_half = half // TILE
    mate = {"pcol": flip(0)}

    def half_at(side, i):
        return pl.ds(pl.multiple_of(side * half + i * TILE, TILE), TILE)

    def tile_of(i):
        return pl.ds(pl.multiple_of(i * TILE, TILE), TILE)

    def red_copy(i):
        return remote(part.at[half_at(1 - h, i)], got.at[0, tile_of(i)], red_send.at[i], red_recv.at[i], mate)

    def times(side, i):
        at = half_at(side, i)
        wide = lax.dot_general(t_hi[at], vcat[...], (((1,), (0,)), ((), ())), preferred_element_type=F32)
        rest = lax.dot_general(t_lo[at], vcat[:, :size], (((1,), (0,)), ((), ())), preferred_element_type=F32)
        part[at] = wide[:, :size] + (wide[:, size:] + rest)

    small_rows = PAIR // 2 * chunk_rows
    tiles = half // small_rows
    last = bits - 1

    def small_at(i):
        return pl.ds(i * small_rows, small_rows)

    def side_at(side, i):
        return pl.ds(pl.multiple_of(side * half + i * small_rows, small_rows), small_rows)

    def bit_copy(bit, i):
        return remote(
            acc.at[bit, small_at(i)], got.at[bit, small_at(i)], bit_send.at[bit, i], bit_recv.at[bit, i],
            {"pcol": flip(bit)},
        )

    def back_copy(i, side):
        at = side_at(side, i)
        return remote(prod.at[at], prod.at[at], back_send.at[i], back_recv.at[i], mate)

    def reduced(i):
        red_copy(i).wait_recv()
        if bits > 1:
            acc[1, tile_of(i)] = part[half_at(h, i)] + got[0, tile_of(i)]
            for j in range(i * TILE // small_rows, (i + 1) * TILE // small_rows):
                bit_copy(1, j).start()

    for i in range(per_half):
        times(1 - h, i)
        red_copy(i).start()
        if i > 0:
            reduced(i - 1)
        times(h, i)
    reduced(per_half - 1)

    def row_vectors(i, carry):
        at = tile_of(i)
        value = pair_dot(split(panel_ref[at]), linv_pair, ((1,), (1,))) + unit(me * rows + i * TILE)
        vec[at] = value
        left_hi[at, :size], left_lo[at, :size] = split(value)
        return carry

    lax.fori_loop(0, rows // TILE, row_vectors, 0)
    small_ref[...] = exact_dot(vec[...], part[...], ((0,), (0,)))
    sends = scatter(small_ref, rs2_ref, rs2_send, rs2_recv)
    for copy in sends:
        copy.start()

    for bit in range(1, last):
        for i in range(tiles):
            bit_copy(bit, i).wait_recv()
            acc[bit + 1, small_at(i)] = acc[bit, small_at(i)] + got[bit, small_at(i)]
            bit_copy(bit + 1, i).start()

    def across(offset):
        to = (q + offset) % m
        return remote(pc_ref.at[q], pc_ref.at[q], pc_send.at[offset], pc_recv.at[offset], {"pcol": to})

    def came(offset):
        slot = pc_ref.at[(q - offset + m) % m]
        return remote(slot, slot, pc_send.at[offset], pc_recv.at[offset], {"pcol": (q + offset) % m})

    crossing = [across(o) for o in range(1, m)]
    for i in range(tiles + 1):
        if i < tiles:
            if bits > 1:
                bit_copy(last, i).wait_recv()
                value = acc[last, small_at(i)] + got[last, small_at(i)]
            else:
                value = part[side_at(h, i)] + got[0, small_at(i)]
            prod[side_at(h, i)] = pair_dot(split(value), coupling_pair, ((1,), (0,)))
            back_copy(i, h).start()
        if i == tiles // 2:
            for copy in sends:
                copy.wait_recv()
            pc_ref[q] = collected(small_ref, rs2_ref)
            for copy in crossing:
                copy.start()
        if i > 0:
            back_copy(i - 1, 1 - h).wait_recv()
            for step in range(PAIR * (i - 1), PAIR * i):
                pump_q(step)
    fill(colq, prod)
    for o in range(1, m):
        came(o).wait_recv()
    value = pc_ref[0]
    for j in range(1, m):
        value = value + pc_ref[j]
    both2[me] = value
    sends2, arrivals = spread(both2, ag2_send, ag2_recv)
    for copy in sends2:
        copy.start()

    def rest(step, carry):
        pump_q(step)
        return carry

    lax.fori_loop(CHUNKS, steps_q, rest, 0)
    for copy in arrivals:
        copy.wait_recv()
    inner = exact_dot(both2[...].reshape(size, size), coupling, ((1,), (0,)))
    small = exact_dot(coupling, inner, ((0,), (0,)))
    small_pair = split(small)

    def row_update(i, carry):
        at = tile_of(i)
        value = prod[at] - pair_dot((left_hi[at, :size], left_lo[at, :size]), small_pair, ((1,), (0,)))
        left_hi[at, size:], left_lo[at, size:] = split(value)
        return carry

    lax.fori_loop(0, rows // TILE, row_update, 0)
    fill_wait(colq, prod)

    for j in range(tiles):
        settle(colq, pump2_send, pump2_recv, paired, range(PAIR * j, PAIR * (j + 1)))

        def col_update(i, carry):
            at = pl.ds(pl.multiple_of(i * half + j * small_rows, small_rows), small_rows)
            right_hi[at, :size], right_lo[at, :size] = split(colq[at])
            return carry

        lax.fori_loop(0, 2 * blocks, col_update, 0)
    for copy in crossing:
        copy.wait_send()
    for copy in sends + sends2:
        copy.wait_send()
    for i in range(per_half):
        red_copy(i).wait_send()
    for i in range(tiles):
        back_copy(i, h).wait_send()
        for bit in range(1, bits):
            bit_copy(bit, i).wait_send()
    drain(colp, pump_send, pump_recv)
    drain(colq, pump2_send, pump2_recv)


def exchange(panel, trailing, n, m, nx):
    rows, size = panel.shape
    cols = trailing.shape[1]
    blocks = cols // rows
    piece, half = size // n, rows // 2
    bits = max(m.bit_length() - 1, 2)
    tiles = half // (PAIR // 2 * (rows // CHUNKS))
    dma = pltpu.SemaphoreType.DMA
    vmem = pl.BlockSpec(memory_space=pltpu.VMEM)
    narrow = jnp.bfloat16
    return pl.pallas_call(
        functools.partial(exchange_kernel, (n, m, nx, blocks)),
        out_shape=[
            jax.ShapeDtypeStruct((rows, 2 * size), narrow),
            jax.ShapeDtypeStruct((rows, 2 * size), narrow),
            jax.ShapeDtypeStruct((cols, 2 * size), narrow),
            jax.ShapeDtypeStruct((cols, 2 * size), narrow),
            jax.ShapeDtypeStruct((size, size), F32),
            jax.ShapeDtypeStruct((rows, cols), F32),
        ],
        in_specs=[vmem, pl.BlockSpec(memory_space=pltpu.HBM)],
        out_specs=[vmem] * 6,
        scratch_shapes=[
            dma,
            dma,
            pltpu.VMEM((cols, size), F32),
            pltpu.VMEM((cols, size), F32),
            pltpu.VMEM((cols, 2 * size), narrow),
            pltpu.VMEM((rows, cols), narrow),
            pltpu.VMEM((rows, cols), narrow),
            pltpu.VMEM((rows, size), F32),
            pltpu.VMEM((bits, half, size), F32),
            pltpu.VMEM((bits, half, size), F32),
            pltpu.VMEM((rows, size), F32),
            pltpu.VMEM((rows, size), F32),
            pltpu.VMEM((size, size), F32),
            pltpu.VMEM((n, piece, size), F32),
            pltpu.VMEM((n, 2, piece, size), F32),
            pltpu.VMEM((size, size), F32),
            pltpu.VMEM((n, piece, size), F32),
            pltpu.VMEM((m, piece, size), F32),
            pltpu.VMEM((n, piece, size), F32),
            dma((n,)), dma,
            dma((n,)), dma((n,)), dma((n,)), dma((n,)),
            dma((n,)), dma((n,)), dma((n,)), dma((n,)),
            dma((m,)), dma((m,)),
            dma((blocks, 4)), dma((blocks, CHUNKS)),
            dma((blocks, 4)), dma((blocks, CHUNKS)),
            dma((half // TILE,)), dma((half // TILE,)),
            dma((bits, tiles)), dma((bits, tiles)),
            dma((tiles,)), dma((tiles,)),
        ],
        compiler_params=pltpu.CompilerParams(
            collective_id=0, has_side_effects=True, vmem_limit_bytes=40 * 1024 * 1024
        ),
        name="exchange",
    )(panel, trailing)


def finish_kernel(t_ref, lh, ll, rh, rl, band_ref, out_ref, band_out):
    dims = (((1,), (1,)), ((), ()))
    wide = out_ref.shape[1]
    at = pl.ds(pl.multiple_of(pl.program_id(0) * wide, wide), wide)

    def one(a, b):
        return lax.dot_general(a, b, dims, preferred_element_type=F32)

    out_ref[...] = t_ref[:, at] - (
        one(lh[...], rh[at]) + (one(lh[...], rl[at]) + one(ll[...], rh[at]))
    )

    @pl.when(pl.program_id(0) == 0)
    def _():
        band_out[...] = band_ref[...]


def finish(trailing, lh, ll, rh, rl, band):
    rows, cols = trailing.shape
    tile = 2 * TILE
    whole = pl.BlockSpec(memory_space=pltpu.VMEM)
    return pl.pallas_call(
        finish_kernel,
        grid=(cols // tile,),
        out_shape=[jax.ShapeDtypeStruct((rows, cols), F32), jax.ShapeDtypeStruct(band.shape, F32)],
        in_specs=[whole] * 6,
        out_specs=[pl.BlockSpec((rows, tile), lambda i: (0, i)), whole],
        compiler_params=pltpu.CompilerParams(vmem_limit_bytes=GRANT),
        name="finish",
    )(trailing, lh, ll, rh, rl, band)


def shards(n, m, nx, panel, trailing):
    lh, ll, rh, rl, band, held = exchange(panel, trailing, n, m, nx)
    return tuple(finish(held, lh, ll, rh, rl, band))


def solution(mesh):
    placed = (P("prow", None), P("prow", "pcol"))
    n, m = mesh.shape["prow"], mesh.shape["pcol"]
    column = [getattr(d, "coords", None) for d in mesh.devices[:, 0]]
    nx = 2 if None in column else len({c[0] for c in column})
    return jax.shard_map(
        functools.partial(shards, n, m, nx),
        mesh=mesh,
        in_specs=placed,
        out_specs=(P("prow", "pcol"), P()),
        check_vma=False,
    )
```

```python
import functools

import jax
import jax.numpy as jnp
from jax import lax
from jax.experimental import pallas as pl
from jax.experimental.pallas import tpu as pltpu
from jax.sharding import PartitionSpec as P

STEPS = 16


def factor_body(gram, top_t, between):
    size = gram.shape[0]
    rows = lax.broadcasted_iota(jnp.int32, (size, size), 0)
    cols = lax.broadcasted_iota(jnp.int32, (size, size), 1)

    def block(turn, carry):
        work, other = carry
        live = size - turn * STEPS
        for k in range(STEPS):
            if k % (STEPS // 2) == 0:
                between(2 * turn + 2 * k // STEPS)
            at_col = cols == k
            below = jnp.logical_and(rows > k, rows < live)
            col = jnp.broadcast_to(work[:, k : k + 1], (size, size))
            row_scale = lax.rsqrt(col[k : k + 1, :])
            row = jnp.where(at_col[:1], 1.0, work[k : k + 1, :]) * row_scale
            low = jnp.where(jnp.logical_and(rows >= k, rows < live), col * row_scale, 0.0)
            work = jnp.where(
                rows == k,
                row,
                jnp.where(below, jnp.where(at_col, 0.0, work) - low * row, work),
            )
            ocol = jnp.broadcast_to(other[:, k : k + 1], (size, size)) + low
            inv = 1.0 / ocol[k : k + 1, :]
            orow = jnp.where(at_col[:1], 1.0, other[k : k + 1, :]) * inv
            other = jnp.where(
                rows == k, orow, jnp.where(at_col, 0.0, other) - ocol * orow
            )
        work = jnp.concatenate([work[STEPS:], work[:STEPS]], axis=0)
        other = jnp.concatenate([other[STEPS:], other[:STEPS]], axis=0)
        return pltpu.roll(work, size - STEPS, 1), pltpu.roll(other, size - STEPS, 1)

    return lax.fori_loop(0, size // STEPS, block, (gram, top_t))


def split_factor(work, other):
    size = work.shape[0]
    rows = lax.broadcasted_iota(jnp.int32, (size, size), 0)
    cols = lax.broadcasted_iota(jnp.int32, (size, size), 1)
    linv = jnp.where(rows >= cols, work, 0.0)
    upper = jnp.where(rows < cols, work, jnp.where(rows == cols, 1.0 / jnp.where(rows == cols, work, 1.0), 0.0))
    coupling = lax.dot_general(
        other, upper, (((1,), (1,)), ((), ())), precision=lax.Precision.HIGHEST, preferred_element_type=jnp.float32
    )
    return linv, upper, coupling

MESH = pl.DeviceIdType.MESH
CHUNKS = 16
EARLY = (1, 4, 4)
SLACK = (4, 4)
TILE = 256
PIECE = 64
PAIR = 4
GRANT = 24 * 1024 * 1024
F32 = jnp.float32


def exact_dot(left, right, dims):
    return lax.dot_general(
        left, right, (dims, ((), ())), precision=lax.Precision.HIGHEST, preferred_element_type=F32
    )


def split(value):
    high = value.astype(jnp.bfloat16)
    return high, (value - high.astype(F32)).astype(jnp.bfloat16)


def pair_dot(left, right, dims):
    (lh, ll), (rh, rl) = left, right

    def one(a, b):
        return lax.dot_general(a, b, (dims, ((), ())), preferred_element_type=F32)

    return one(lh, rh) + (one(lh, rl) + one(ll, rh))


def exchange_kernel(
    sizes, panel_ref, trail_ref, left_hi, left_lo, right_hi, right_lo, band_ref, t_buf,
    own_sem, t_sem, colp, colq, vcat, t_hi, t_lo, part, acc, got, prod, vec,
    gram_ref, rs_ref, both, small_ref, rs2_ref, pc_ref, both2,
    top_send, top_recv, rs_send, rs_recv, ag_send, ag_recv, rs2_send, rs2_recv, ag2_send, ag2_recv, pc_send, pc_recv,
    pump_send, pump_recv, pump2_send, pump2_recv, red_send, red_recv, bit_send, bit_recv, back_send, back_recv,
):
    n, m, nx, blocks = sizes
    nz = n // nx
    rows, size = panel_ref.shape
    piece = size // n
    half = rows // 2
    chunk_rows = rows // CHUNKS
    me = lax.axis_index("prow")
    q = lax.axis_index("pcol")
    z, x = me // nx, me % nx
    bits = m.bit_length() - 1

    def flip(bit):
        step = 1 << bit
        return q + step - 2 * step * ((q // step) % 2)

    def peer(offset):
        return (me + offset) % n

    def remote(src, dst, send, recv, where):
        return pltpu.make_async_remote_copy(
            src_ref=src, dst_ref=dst, send_sem=send, recv_sem=recv, device_id=where, device_id_type=MESH
        )

    t_copy = pltpu.make_async_copy(trail_ref, t_buf, t_sem)
    t_copy.start()
    barrier = pltpu.get_barrier_semaphore()
    for offset in range(1, n):
        pl.semaphore_signal(barrier, inc=1, device_id={"prow": peer(offset)}, device_id_type=MESH)
    for offset in range(1, m):
        pl.semaphore_signal(barrier, inc=1, device_id={"pcol": (q + offset) % m}, device_id_type=MESH)

    def place(k):
        b = q * blocks + k
        return b, z - b // nx, x - b % nx

    def filled(buf, source):
        copies = []
        for k in range(blocks):
            b, _, _ = place(k)
            copies.append((me == b, pltpu.make_async_copy(source, buf.at[pl.ds(k * rows, rows)], own_sem)))
        return copies

    def fill(buf, source):
        for mine, copy in filled(buf, source):
            pl.when(mine)(copy.start)

    def fill_wait(buf, source):
        for mine, copy in filled(buf, source):
            pl.when(mine)(copy.wait)

    fill(colp, panel_ref)
    gram_ref[...] = exact_dot(panel_ref[...], panel_ref[...], ((0,), (0,)))
    fill_wait(colp, panel_ref)
    pl.semaphore_wait(barrier, n - 1 + m - 1)

    def children(dz, dx):
        return (
            (jnp.logical_and(jnp.logical_and(dx == 0, dz >= 0), z < nz - 1), me + nx),
            (jnp.logical_and(jnp.logical_and(dx == 0, dz <= 0), z > 0), me - nx),
            (jnp.logical_and(dx >= 0, x < nx - 1), me + 1),
            (jnp.logical_and(dx <= 0, x > 0), me - 1),
        )

    def relays(dz, dx):
        flags = [has for has, _ in children(dz, dx)]
        return functools.reduce(jnp.logical_or, flags)

    def in_order(k, c):
        return pl.multiple_of(c * chunk_rows, chunk_rows)

    def paired(k, c):
        first = place(k)[0] // blocks % 2
        side = (first + c % PAIR // (PAIR // 2)) % 2
        at = side * half + c // PAIR * (PAIR // 2) * chunk_rows + c % (PAIR // 2) * chunk_rows
        return pl.multiple_of(at, chunk_rows)

    def settle(buf, send, recv, where, span):
        for k in range(blocks):
            _, dz, dx = place(k)
            away = jnp.logical_or(dz != 0, dx != 0)

            @pl.when(jnp.logical_and(away, jnp.logical_not(relays(dz, dx))))
            def _():
                for c in span:
                    part_of = buf.at[pl.ds(k * rows + where(k, c), chunk_rows)]
                    remote(part_of, part_of, send.at[k, 0], recv.at[k, c], {"prow": peer(1)}).wait_recv()

    def pump(step, buf, source, send, recv, where, slack):
        for k in range(blocks):
            _, dz, dx = place(k)
            far = jnp.where(dz < 0, -dz, dz) + jnp.where(dx < 0, -dx, dx)
            c = step - slack * far

            @pl.when(jnp.logical_and(c >= 0, c < CHUNKS))
            def _():
                part_of = buf.at[pl.ds(k * rows + where(k, c), chunk_rows)]

                @pl.when(jnp.logical_and(far > 0, relays(dz, dx)))
                def _():
                    remote(part_of, part_of, send.at[k, 0], recv.at[k, c], {"prow": peer(1)}).wait_recv()

                for d, (has, to) in enumerate(children(dz, dx)):

                    @pl.when(has if source is None else jnp.logical_and(has, far > 0))
                    def _():
                        remote(part_of, part_of, send.at[k, d], recv.at[k, c], {"prow": to}).start()

                    if source is not None:

                        @pl.when(jnp.logical_and(has, far == 0))
                        def _():
                            own = source.at[pl.ds(where(k, c), chunk_rows)]
                            remote(own, part_of, send.at[k, d], recv.at[k, c], {"prow": to}).start()

    def pump_p(step):
        pump(step, colp, None, pump_send, pump_recv, in_order, SLACK[0])

    def pump_q(step):
        pump(step, colq, prod, pump2_send, pump2_recv, paired, SLACK[1])

    def drain(buf, send, recv):
        for k in range(blocks):
            _, dz, dx = place(k)
            whole = buf.at[pl.ds(k * rows, rows)]
            for d, (has, to) in enumerate(children(dz, dx)):

                @pl.when(has)
                def _():
                    remote(whole, whole, send.at[k, d], recv.at[k, 0], {"prow": peer(1)}).wait_send()

    steps_p, steps_q = [CHUNKS + slack * (nz - 1 + max(nx - 1, 0)) for slack in SLACK]

    def scatter(src, slots, send, recv):
        def copy(offset):
            to = peer(offset)
            return remote(
                src.at[pl.ds(to * piece, piece)], slots.at[offset], send.at[offset], recv.at[offset], {"prow": to}
            )

        return [copy(offset) for offset in range(1, n)]

    def spread(slots, send, recv):
        def copy(offset):
            return remote(slots.at[me], slots.at[me], send.at[offset], recv.at[offset], {"prow": peer(offset)})

        def arrive(offset):
            slot = slots.at[peer(n - offset)]
            return remote(slot, slot, send.at[offset], recv.at[offset], {"prow": peer(offset)})

        return [copy(o) for o in range(1, n)], [arrive(o) for o in range(1, n)]

    def collected(src, slots):
        value = src[pl.ds(me * piece, piece)]
        for offset in range(1, n):
            value = value + slots[offset]
        return value

    def split_rows(side):
        def body(i, carry):
            at = pl.ds(pl.multiple_of(side * half + i * PIECE, PIECE), PIECE)
            t_hi[at], t_lo[at] = split(t_buf[at])
            return carry

        lax.fori_loop(0, half // PIECE, body, 0)

    def top_copy(j):
        return remote(panel_ref.at[pl.ds(j * piece, piece)], both.at[j, 1], top_send.at[j], top_recv, {"prow": j})

    @pl.when(me == 0)
    def _():
        for j in range(1, n):
            top_copy(j).start()
        both[0, 1] = panel_ref[:piece]

    for step in range(EARLY[0]):
        pump_p(step)
    sends = scatter(gram_ref, rs_ref, rs_send, rs_recv)
    for copy in sends:
        copy.start()
    for step in range(EARLY[0], sum(EARLY[:2])):
        pump_p(step)
    t_copy.wait()
    split_rows(0)

    @pl.when(me > 0)
    def _():
        slot = both.at[me, 1]
        remote(slot, slot, top_send.at[0], top_recv, {"prow": peer(1)}).wait_recv()

    for copy in sends:
        copy.wait_recv()
    both[me, 0] = collected(gram_ref, rs_ref)
    sends2, arrivals = spread(both, ag_send, ag_recv)
    for copy in sends2:
        copy.start()
    for step in range(sum(EARLY[:2]), sum(EARLY)):
        pump_p(step)
    split_rows(1)
    for copy in arrivals:
        copy.wait_recv()
    for copy in sends + sends2:
        copy.wait_send()

    @pl.when(me == 0)
    def _():
        for j in range(1, n):
            top_copy(j).wait_send()

    done = sum(EARLY)
    turns = 2 * (size // STEPS)
    work, other = factor_body(
        both[:, 0].reshape(size, size),
        both[:, 1].reshape(size, size).T,
        lambda turn: pump_p(done + turn),
    )
    for step in range(done + turns, steps_p):
        pump_p(step)
    settle(colp, pump_send, pump_recv, in_order, range(CHUNKS))
    linv, upper, coupling = split_factor(work, other)
    band_ref[...] = -upper
    linv_pair = split(linv)
    coupling_pair = split(coupling)

    def unit(start):
        r = lax.broadcasted_iota(jnp.int32, (TILE, size), 0) + start
        return jnp.where(r == lax.broadcasted_iota(jnp.int32, (TILE, size), 1), 1.0, 0.0)

    def col_vectors(i, carry):
        at = pl.ds(pl.multiple_of(i * TILE, TILE), TILE)
        value = pair_dot(split(colp[at]), linv_pair, ((1,), (1,))) + unit(q * blocks * rows + i * TILE)
        high, low = split(value)
        vcat[at, :size] = high
        vcat[at, size:] = low
        right_hi[at, size:] = high
        right_lo[at, size:] = low
        return carry

    lax.fori_loop(0, blocks * rows // TILE, col_vectors, 0)

    h = q % 2
    per_half = half // TILE
    mate = {"pcol": flip(0)}

    def half_at(side, i):
        return pl.ds(pl.multiple_of(side * half + i * TILE, TILE), TILE)

    def tile_of(i):
        return pl.ds(pl.multiple_of(i * TILE, TILE), TILE)

    def red_copy(i):
        return remote(part.at[half_at(1 - h, i)], got.at[0, tile_of(i)], red_send.at[i], red_recv.at[i], mate)

    def times(side, i):
        at = half_at(side, i)
        wide = lax.dot_general(t_hi[at], vcat[...], (((1,), (0,)), ((), ())), preferred_element_type=F32)
        rest = lax.dot_general(t_lo[at], vcat[:, :size], (((1,), (0,)), ((), ())), preferred_element_type=F32)
        part[at] = wide[:, :size] + (wide[:, size:] + rest)

    small_rows = PAIR // 2 * chunk_rows
    tiles = half // small_rows
    last = bits - 1

    def small_at(i):
        return pl.ds(i * small_rows, small_rows)

    def side_at(side, i):
        return pl.ds(pl.multiple_of(side * half + i * small_rows, small_rows), small_rows)

    def bit_copy(bit, i):
        return remote(
            acc.at[bit, small_at(i)], got.at[bit, small_at(i)], bit_send.at[bit, i], bit_recv.at[bit, i],
            {"pcol": flip(bit)},
        )

    def back_copy(i, side):
        at = side_at(side, i)
        return remote(prod.at[at], prod.at[at], back_send.at[i], back_recv.at[i], mate)

    def reduced(i):
        red_copy(i).wait_recv()
        if bits > 1:
            acc[1, tile_of(i)] = part[half_at(h, i)] + got[0, tile_of(i)]
            for j in range(i * TILE // small_rows, (i + 1) * TILE // small_rows):
                bit_copy(1, j).start()

    for i in range(per_half):
        times(1 - h, i)
        red_copy(i).start()
        if i > 0:
            reduced(i - 1)
        times(h, i)
    reduced(per_half - 1)

    def row_vectors(i, carry):
        at = tile_of(i)
        value = pair_dot(split(panel_ref[at]), linv_pair, ((1,), (1,))) + unit(me * rows + i * TILE)
        vec[at] = value
        left_hi[at, :size], left_lo[at, :size] = split(value)
        return carry

    lax.fori_loop(0, rows // TILE, row_vectors, 0)
    small_ref[...] = exact_dot(vec[...], part[...], ((0,), (0,)))
    sends = scatter(small_ref, rs2_ref, rs2_send, rs2_recv)
    for copy in sends:
        copy.start()

    for bit in range(1, last):
        for i in range(tiles):
            bit_copy(bit, i).wait_recv()
            acc[bit + 1, small_at(i)] = acc[bit, small_at(i)] + got[bit, small_at(i)]
            bit_copy(bit + 1, i).start()

    def across(offset):
        to = (q + offset) % m
        return remote(pc_ref.at[q], pc_ref.at[q], pc_send.at[offset], pc_recv.at[offset], {"pcol": to})

    def came(offset):
        slot = pc_ref.at[(q - offset + m) % m]
        return remote(slot, slot, pc_send.at[offset], pc_recv.at[offset], {"pcol": (q + offset) % m})

    crossing = [across(o) for o in range(1, m)]
    for i in range(tiles + 1):
        if i < tiles:
            if bits > 1:
                bit_copy(last, i).wait_recv()
                value = acc[last, small_at(i)] + got[last, small_at(i)]
            else:
                value = part[side_at(h, i)] + got[0, small_at(i)]
            prod[side_at(h, i)] = pair_dot(split(value), coupling_pair, ((1,), (0,)))
            back_copy(i, h).start()
        if i == tiles // 2:
            for copy in sends:
                copy.wait_recv()
            pc_ref[q] = collected(small_ref, rs2_ref)
            for copy in crossing:
                copy.start()
        if i > 0:
            back_copy(i - 1, 1 - h).wait_recv()
            for step in range(PAIR * (i - 1), PAIR * i):
                pump_q(step)
    fill(colq, prod)
    for o in range(1, m):
        came(o).wait_recv()
    value = pc_ref[0]
    for j in range(1, m):
        value = value + pc_ref[j]
    both2[me] = value
    sends2, arrivals = spread(both2, ag2_send, ag2_recv)
    for copy in sends2:
        copy.start()

    def rest(step, carry):
        pump_q(step)
        return carry

    lax.fori_loop(CHUNKS, steps_q, rest, 0)
    for copy in arrivals:
        copy.wait_recv()
    inner = exact_dot(both2[...].reshape(size, size), coupling, ((1,), (0,)))
    small = exact_dot(coupling, inner, ((0,), (0,)))
    small_pair = split(small)

    def row_update(i, carry):
        at = tile_of(i)
        value = prod[at] - pair_dot((left_hi[at, :size], left_lo[at, :size]), small_pair, ((1,), (0,)))
        left_hi[at, size:], left_lo[at, size:] = split(value)
        return carry

    lax.fori_loop(0, rows // TILE, row_update, 0)
    fill_wait(colq, prod)

    for j in range(tiles):
        settle(colq, pump2_send, pump2_recv, paired, range(PAIR * j, PAIR * (j + 1)))

        def col_update(i, carry):
            at = pl.ds(pl.multiple_of(i * half + j * small_rows, small_rows), small_rows)
            right_hi[at, :size], right_lo[at, :size] = split(colq[at])
            return carry

        lax.fori_loop(0, 2 * blocks, col_update, 0)
    for copy in crossing:
        copy.wait_send()
    for copy in sends + sends2:
        copy.wait_send()
    for i in range(per_half):
        red_copy(i).wait_send()
    for i in range(tiles):
        back_copy(i, h).wait_send()
        for bit in range(1, bits):
            bit_copy(bit, i).wait_send()
    drain(colp, pump_send, pump_recv)
    drain(colq, pump2_send, pump2_recv)


def exchange(panel, trailing, n, m, nx):
    rows, size = panel.shape
    cols = trailing.shape[1]
    blocks = cols // rows
    piece, half = size // n, rows // 2
    bits = max(m.bit_length() - 1, 2)
    tiles = half // (PAIR // 2 * (rows // CHUNKS))
    dma = pltpu.SemaphoreType.DMA
    vmem = pl.BlockSpec(memory_space=pltpu.VMEM)
    narrow = jnp.bfloat16
    return pl.pallas_call(
        functools.partial(exchange_kernel, (n, m, nx, blocks)),
        out_shape=[
            jax.ShapeDtypeStruct((rows, 2 * size), narrow),
            jax.ShapeDtypeStruct((rows, 2 * size), narrow),
            jax.ShapeDtypeStruct((cols, 2 * size), narrow),
            jax.ShapeDtypeStruct((cols, 2 * size), narrow),
            jax.ShapeDtypeStruct((size, size), F32),
            jax.ShapeDtypeStruct((rows, cols), F32),
        ],
        in_specs=[vmem, pl.BlockSpec(memory_space=pltpu.HBM)],
        out_specs=[vmem] * 6,
        scratch_shapes=[
            dma,
            dma,
            pltpu.VMEM((cols, size), F32),
            pltpu.VMEM((cols, size), F32),
            pltpu.VMEM((cols, 2 * size), narrow),
            pltpu.VMEM((rows, cols), narrow),
            pltpu.VMEM((rows, cols), narrow),
            pltpu.VMEM((rows, size), F32),
            pltpu.VMEM((bits, half, size), F32),
            pltpu.VMEM((bits, half, size), F32),
            pltpu.VMEM((rows, size), F32),
            pltpu.VMEM((rows, size), F32),
            pltpu.VMEM((size, size), F32),
            pltpu.VMEM((n, piece, size), F32),
            pltpu.VMEM((n, 2, piece, size), F32),
            pltpu.VMEM((size, size), F32),
            pltpu.VMEM((n, piece, size), F32),
            pltpu.VMEM((m, piece, size), F32),
            pltpu.VMEM((n, piece, size), F32),
            dma((n,)), dma,
            dma((n,)), dma((n,)), dma((n,)), dma((n,)),
            dma((n,)), dma((n,)), dma((n,)), dma((n,)),
            dma((m,)), dma((m,)),
            dma((blocks, 4)), dma((blocks, CHUNKS)),
            dma((blocks, 4)), dma((blocks, CHUNKS)),
            dma((half // TILE,)), dma((half // TILE,)),
            dma((bits, tiles)), dma((bits, tiles)),
            dma((tiles,)), dma((tiles,)),
        ],
        compiler_params=pltpu.CompilerParams(
            collective_id=0, has_side_effects=True, vmem_limit_bytes=40 * 1024 * 1024
        ),
        name="exchange",
    )(panel, trailing)


def finish_kernel(t_ref, lh, ll, rh, rl, band_ref, out_ref, band_out):
    dims = (((1,), (1,)), ((), ()))
    wide = out_ref.shape[1]
    at = pl.ds(pl.multiple_of(pl.program_id(0) * wide, wide), wide)

    def one(a, b):
        return lax.dot_general(a, b, dims, preferred_element_type=F32)

    out_ref[...] = t_ref[:, at] - (
        one(lh[...], rh[at]) + (one(lh[...], rl[at]) + one(ll[...], rh[at]))
    )

    @pl.when(pl.program_id(0) == 0)
    def _():
        band_out[...] = band_ref[...]


def finish(trailing, lh, ll, rh, rl, band):
    rows, cols = trailing.shape
    tile = 2 * TILE
    whole = pl.BlockSpec(memory_space=pltpu.VMEM)
    return pl.pallas_call(
        finish_kernel,
        grid=(cols // tile,),
        out_shape=[jax.ShapeDtypeStruct((rows, cols), F32), jax.ShapeDtypeStruct(band.shape, F32)],
        in_specs=[whole] * 6,
        out_specs=[pl.BlockSpec((rows, tile), lambda i: (0, i)), whole],
        compiler_params=pltpu.CompilerParams(vmem_limit_bytes=GRANT),
        name="finish",
    )(trailing, lh, ll, rh, rl, band)


def shards(n, m, nx, panel, trailing):
    lh, ll, rh, rl, band, held = exchange(panel, trailing, n, m, nx)
    return tuple(finish(held, lh, ll, rh, rl, band))


def solution(mesh):
    placed = (P("prow", None), P("prow", "pcol"))
    n, m = mesh.shape["prow"], mesh.shape["pcol"]
    column = [getattr(d, "coords", None) for d in mesh.devices[:, 0]]
    nx = 2 if None in column else len({c[0] for c in column})
    return jax.shard_map(
        functools.partial(shards, n, m, nx),
        mesh=mesh,
        in_specs=placed,
        out_specs=(P("prow", "pcol"), P()),
        check_vma=False,
    )
```
